32 devices in a mesh: src: 4 (over y, x), tgt: 8 (over z, core).
Axes of the slice: x: 2, y: 2, z: 4, core: 2. Of those that a mesh axis runs over, the one named last changes fastest.
Arguments:
- source_pca: float32 [64, 16384], P(None, 'src'), may hold values from -6 to 6
- target_pca: float32 [64, 8192], P(None, 'tgt'), may hold values from -6 to 6
- source_labels: int32 [16384], P('src'), may hold values from 0 to 63, as said below
- target_labels: int32 [8192], P('tgt'), may hold values from 0 to 63, as said below
- block_mask: int32 [64, 64], replicated, may hold values from 0 to 1, as said below
Outputs:
- source_projection: float32 [64, 16384], P(None, ('src', 'tgt'))
- target_projection: float32 [64, 8192], P(None, 'tgt')
The draws below stay inside these ranges and needn't reach their ends.
Inputs may be any that keep to these rules, and one draw needn't show every extreme that they name: `source_labels`: each aligned block of 4096 consecutive source cells holds every one of the 64 clusters. `target_labels`: each aligned block of 1024 consecutive target cells holds every one of the 64 clusters. `block_mask`: entries are 0 or 1, and the diagonal is all ones.
All inputs are finite; a program needn't handle non-finite values.
Results may differ from the reference program's by a relative error of at most 0.0003.
Values sent between devices are 32-bit elements; how exact they have to be, the bound alone decides.
No kernel may reach another device: no remote copies, remote signals or barrier semaphores. Data moves between devices by JAX's collectives and lax.ppermute only.
A program may use at most 64 MiB of HBM per device.

```python
import math
import jax
import jax.numpy as jnp
from jax import lax

D = 64
K = 64
ITERS = 2
RS = 4096
CT = 1024
NS = 16384
NT = 8192


def covered_labels(key, total, block):
    shards = total // block
    keys = jax.random.split(key, 3)
    labels = jax.random.randint(keys[0], (shards, block), 0, K)
    cover = jax.vmap(lambda k: jax.random.permutation(k, K))(jax.random.split(keys[1], shards))
    labels = labels.at[:, :K].set(cover)
    labels = jax.vmap(lambda k, row: jax.random.permutation(k, row))(jax.random.split(keys[2], shards), labels)
    return labels.reshape(total).astype(jnp.int32)


def draw_source_labels(key, part):
    return covered_labels(jax.random.fold_in(key, 11), NS, RS)


def draw_target_labels(key, part):
    return covered_labels(jax.random.fold_in(key, 23), NT, CT)


def draw_block_mask(key, part):
    picks = jax.random.randint(jax.random.fold_in(key, 37), (K, K), 0, 4) == 0
    diagonal = jnp.arange(K)[:, None] == jnp.arange(K)[None, :]
    return jnp.where(picks | diagonal, 1, 0).astype(jnp.int32)


def draw_source_pca(key, part):
    keys = jax.random.split(jax.random.fold_in(key, 53), 1)
    values = jnp.clip(jax.random.normal(keys[0], (D, NS), jnp.float32), -6.0, 6.0)
    return values.astype(jnp.float32)


def block_levels(stream_key, dims, pieces, least, high):
    def one(axis_at, blocks):
        steps = jax.random.uniform(jax.random.fold_in(jax.random.fold_in(stream_key, 6), axis_at), (blocks,), jnp.float32, least / len(pieces), high / len(pieces))
        return jnp.repeat(jnp.exp(steps), dims[axis_at] // blocks).reshape((-1,) + (1,) * (len(dims) - axis_at - 1))

    loudness = one(*pieces[0])
    for cut in pieces[1:]:
        loudness = loudness * one(*cut)
    return loudness


def noise(key, shape, scale, reach, cuts=(), dtype=jnp.bfloat16):
    level = block_levels(key, shape, cuts, -0.22, 0.18) if cuts else 1.0
    result = jax.random.normal(key, shape, jnp.float32) * scale * level
    return jnp.minimum(jnp.maximum(result, -reach), reach).astype(dtype)


def setup_inputs(seed: int = 0) -> dict:
    key_of = jax.random.split(jax.random.key(seed), 6)
    source_pca = draw_source_pca(jax.random.fold_in(key_of[5], 71), 0)
    target_pca = noise(key_of[1], (D, NT), 1.0, 6.0, ((1, 8),), jnp.float32)
    source_labels = draw_source_labels(jax.random.fold_in(key_of[5], 71), 0)
    target_labels = draw_target_labels(jax.random.fold_in(key_of[5], 71), 0)
    block_mask = draw_block_mask(jax.random.fold_in(key_of[5], 71), 0)
    return {"source_pca": source_pca, "target_pca": target_pca, "source_labels": source_labels, "target_labels": target_labels, "block_mask": block_mask}


EPSILON = 0.05
FLOOR = -1.0e30


def costs(xb, yt):
    cross = lax.dot_general(xb, yt, (((0,), (0,)), ((), ())), precision=lax.Precision.HIGHEST)
    return (jnp.sum(xb * xb, 0)[:, None] + jnp.sum(yt * yt, 0)[None, :] - 2.0 * cross) / D


def reference(source_pca, target_pca, source_labels, target_labels, block_mask):
    rblock = min(512, RS)
    nblock = NS // rblock
    xblocks = source_pca.reshape(D, nblock, rblock).transpose(1, 0, 2)
    lblocks = source_labels.reshape(nblock, rblock)

    def logits(xb, lab, shift_rows, shift_cols):
        allowed = block_mask[lab][:, target_labels] > 0
        value = (shift_rows[:, None] + shift_cols[None, :] - costs(xb, target_pca)) / EPSILON
        return jnp.where(allowed, value, -jnp.inf)

    zero_rows = jnp.zeros((rblock,), jnp.float32)
    zero_cols = jnp.zeros((NT,), jnp.float32)
    g_pot = jnp.zeros((NT,), jnp.float32)
    f_pot = jnp.zeros((NS,), jnp.float32)
    for step in range(ITERS):
        def row_pass(item):
            xb, lab = item
            z = logits(xb, lab, zero_rows, g_pot)
            peak = jnp.max(z, 1)
            return peak + jnp.log(jnp.sum(jnp.exp(z - peak[:, None]), 1))

        lse = lax.map(row_pass, (xblocks, lblocks)).reshape(NS)
        f_pot = -EPSILON * math.log(NS) - EPSILON * lse
        fblocks = f_pot.reshape(nblock, rblock)

        def col_step(carry, item):
            peak, total = carry
            xb, lab, fb = item
            z = logits(xb, lab, fb, zero_cols)
            newer = jnp.maximum(peak, jnp.max(z, 0))
            total = total * jnp.exp(peak - newer) + jnp.sum(jnp.exp(z - newer[None, :]), 0)
            return (newer, total), None

        init = (jnp.full((NT,), FLOOR, jnp.float32), jnp.zeros((NT,), jnp.float32))
        (peak, total), unused = lax.scan(col_step, init, (xblocks, lblocks, fblocks))
        g_pot = -EPSILON * math.log(NT) - EPSILON * (peak + jnp.log(total))

    fblocks = f_pot.reshape(nblock, rblock)

    def proj_step(carry, item):
        peak, total, weighted = carry
        xb, lab, fb = item
        z = logits(xb, lab, fb, g_pot)
        rpeak = jnp.max(z, 1)
        rprob = jnp.exp(z - rpeak[:, None])
        rows = lax.dot_general(target_pca, rprob, (((1,), (1,)), ((), ())), precision=lax.Precision.HIGHEST)
        rows = rows / jnp.sum(rprob, 1)[None, :]
        newer = jnp.maximum(peak, jnp.max(z, 0))
        cprob = jnp.exp(z - newer[None, :])
        scale = jnp.exp(peak - newer)
        total = total * scale + jnp.sum(cprob, 0)
        weighted = weighted * scale[None, :] + jnp.dot(xb, cprob, precision=lax.Precision.HIGHEST)
        return (newer, total, weighted), rows

    init = (jnp.full((NT,), FLOOR, jnp.float32), jnp.zeros((NT,), jnp.float32), jnp.zeros((D, NT), jnp.float32))
    (peak, total, weighted), rows = lax.scan(proj_step, init, (xblocks, lblocks, fblocks))
    source_projection = rows.transpose(1, 0, 2).reshape(D, NS)
    target_projection = weighted / total[None, :]
    return source_projection, target_projection
```

```python
import functools
import math

import jax
import jax.numpy as jnp
from jax import lax
from jax.experimental import pallas as pl
from jax.experimental.pallas import tpu as pltpu
from jax.sharding import PartitionSpec as P

ITERS = 2
EPSILON = 0.05
BARRED = -(2.0**100)
LANES = 128
LOG2E = math.log2(math.e)
F32 = jnp.float32
BF16 = jnp.bfloat16
VMEM = pl.BlockSpec(memory_space=pltpu.VMEM)


def halves(value):
    high = value.astype(BF16)
    low = (value - high.astype(F32)).astype(BF16)
    return high, low


def onehot(labels, clusters):
    series = lax.broadcasted_iota(jnp.int32, (clusters, labels.shape[1]), 0)
    return series == labels


def barred_by(mask_ref, hot, transposed):
    stop = (1.0 - mask_ref[...].astype(F32)).astype(BF16)
    dims = (((0,), (0,)), ((), ())) if transposed else (((1,), (0,)), ((), ()))
    picked = lax.dot_general(stop, hot.astype(BF16), dims, preferred_element_type=F32)
    return picked * BARRED


def tree(combine, parts):
    parts = list(parts)
    while len(parts) > 1:
        parts = [
            combine(parts[k], parts[k + 1]) if k + 1 < len(parts) else parts[k]
            for k in range(0, len(parts), 2)
        ]
    return parts[0]


def merge(tops):
    peak = tree(jnp.maximum, tops)
    return peak + jnp.log2(tree(jnp.add, [jnp.exp2(part - peak) for part in tops]))


def to_rows(line_ref, wide):
    for k in range(line_ref.shape[0]):
        line_ref[k : k + 1, :] = wide[:, k * LANES : (k + 1) * LANES]


def spread_lanes(dst_ref, rows):
    for k in range(rows.shape[0]):
        square = jnp.broadcast_to(rows[k : k + 1, :], (LANES, LANES))
        dst_ref[k * LANES : (k + 1) * LANES, :] = square.T


def gather_lanes(dst_ref, column_ref):
    for k in range(dst_ref.shape[0]):
        dst_ref[k : k + 1, :] = column_ref[k * LANES : (k + 1) * LANES, :].T[0:1, :]


def row_sweep(cross_ref, shift_ref, lse_ref, width=512, depth=64):
    cols, rows = cross_ref.shape
    per = width // LANES

    def block(q, unused):
        lanes = pl.multiple_of(q * width, width)

        def step(s, carry):
            start = pl.multiple_of(s * depth, depth)
            peaks, sums = carry
            shift = [shift_ref[pl.ds(start + 8 * r, 8), :] for r in range(depth // 8)]
            new_peaks, new_sums = [], []
            for p in range(per):
                at = pl.multiple_of(lanes + p * LANES, LANES)
                z = [
                    cross_ref[pl.ds(start + 8 * r, 8), pl.ds(at, LANES)] + shift[r]
                    for r in range(depth // 8)
                ]
                peak = jnp.maximum(peaks[p], tree(jnp.maximum, z))
                total = tree(jnp.add, [jnp.exp2(part - peak) for part in z])
                new_peaks.append(peak)
                new_sums.append(sums[p] * jnp.exp2(peaks[p] - peak) + total)
            return new_peaks, new_sums

        peaks, sums = lax.fori_loop(
            0,
            cols // depth,
            step,
            (
                [jnp.full((8, LANES), 2.0 * BARRED, F32)] * per,
                [jnp.zeros((8, LANES), F32)] * per,
            ),
        )
        for p in range(per):
            peak = jnp.max(peaks[p], 0, keepdims=True)
            total = jnp.sum(sums[p] * jnp.exp2(peaks[p] - peak), 0, keepdims=True)
            lse_ref[pl.ds(q * per + p, 1), :] = peak + jnp.log2(total)
        return unused

    lax.fori_loop(0, rows // width, block, 0)


def make_operands(x, hot, other, parts):
    high, low = halves(x)
    parts[...] = jnp.concatenate([high, low, high, hot.astype(BF16)], 0)


def first_kernel(
    scale, eps_scale, x_ref, y_ref, sl_ref, tl_ref, mask_ref,
    cross_ref, lse_ref, xsq_ref, xop_ref, yop_ref, ysq_ref, none_ref,
):
    dims, rows = x_ref.shape
    cols = y_ref.shape[1]
    clusters = mask_ref.shape[0]
    high, low = halves(y_ref[...] * scale)
    barred = barred_by(mask_ref, onehot(tl_ref[...], clusters), False)
    stacked = jnp.concatenate([high.astype(F32), high.astype(F32), low.astype(F32), barred], 0)
    yop_ref[...] = stacked.T.astype(BF16)
    ysq = jnp.sum(y_ref[...] * y_ref[...], 0, keepdims=True) * (-eps_scale)
    for k in range(cols // LANES):
        square = jnp.broadcast_to(ysq[:, k * LANES : (k + 1) * LANES], (LANES, LANES))
        ysq_ref[k * LANES : (k + 1) * LANES, :] = square.T
    none_ref[...] = jnp.zeros_like(none_ref)
    width = min(256, rows)

    def chunk(q, unused):
        at = pl.ds(pl.multiple_of(q * width, width), width)
        x = x_ref[:, at]
        high, low = halves(x)
        hot = onehot(sl_ref[:, at], clusters).astype(BF16)
        xop_ref[...] = jnp.concatenate([high, low, high, hot], 0)
        xsq = jnp.sum(x * x, 0, keepdims=True) * eps_scale
        for p in range(width // LANES):
            xsq_ref[pl.ds(q * (width // LANES) + p, 1), :] = xsq[:, p * LANES : (p + 1) * LANES]
        cross = jnp.dot(yop_ref[...], xop_ref[...], preferred_element_type=F32)
        for p in range(width // LANES):
            cross_ref[:, pl.ds(pl.multiple_of(q * width + p * LANES, LANES), LANES)] = (
                cross[:, p * LANES : (p + 1) * LANES] + ysq_ref[...]
            )
        return unused

    lax.fori_loop(0, rows // width, chunk, 0)
    row_sweep(cross_ref, none_ref, lse_ref)


def source_shift(parts_refs, xsq_ref, total_rows):
    lse = merge([ref[...] for ref in parts_refs]) - xsq_ref[...]
    pot = -math.log2(total_rows) - lse
    return pot - xsq_ref[...]


def column_peaks(cross_ref, shift, peak_at):
    pass


def col_kernel(total_rows, n_parts, cross_ref, xsq_ref, *refs):
    parts, (lse_ref, shift_ref, column_ref) = refs[:n_parts], refs[n_parts:]
    cols, rows = cross_ref.shape
    shift = source_shift(parts, xsq_ref, total_rows)
    for k in range(rows // LANES):
        shift_ref[:, k * LANES : (k + 1) * LANES] = jnp.broadcast_to(
            shift[k : k + 1, :], (8, LANES)
        )
    deep = min(16, rows // LANES)
    groups = 2

    def block(q, unused):
        for r in range(groups):
            start = pl.multiple_of((q * groups + r) * 8, 8)
            peak = jnp.full((8, LANES), 2.0 * BARRED, F32)
            total = jnp.zeros((8, LANES), F32)
            for c in range(rows // LANES // deep):
                z = [
                    cross_ref[pl.ds(start, 8), (c * deep + k) * LANES : (c * deep + k + 1) * LANES]
                    + shift_ref[:, (c * deep + k) * LANES : (c * deep + k + 1) * LANES]
                    for k in range(deep)
                ]
                newer = jnp.maximum(peak, tree(jnp.maximum, z))
                fresh = tree(jnp.add, [jnp.exp2(part - newer) for part in z])
                total = total * jnp.exp2(peak - newer) + fresh
                peak = newer
            top = jnp.max(peak, 1, keepdims=True)
            mass = jnp.sum(total * jnp.exp2(peak - top), 1, keepdims=True)
            column_ref[pl.ds(start, 8), :] = jnp.broadcast_to(top + jnp.log2(mass), (8, LANES))
        return unused

    lax.fori_loop(0, cols // 8 // groups, block, 0)
    gather_lanes(lse_ref, column_ref)


def target_potential(parts_refs, total_cols):
    return -math.log2(total_cols) - merge([ref[...] for ref in parts_refs])


def row_kernel(total_cols, n_parts, cross_ref, *refs):
    parts, (lse_ref, shift_ref) = refs[:n_parts], refs[n_parts:]
    spread_lanes(shift_ref, target_potential(parts, total_cols))
    row_sweep(cross_ref, shift_ref, lse_ref)


def last_col_kernel(total_rows, n_parts, cross_ref, xsq_ref, x_ref, *refs):
    parts = refs[:n_parts]
    lse_ref, weight_ref, shift_ref, peak_ref, mass_ref, xst_ref, acc_ref = refs[n_parts:]
    cols, rows = cross_ref.shape
    dims = x_ref.shape[0]
    shift = source_shift(parts, xsq_ref, total_rows)
    for k in range(rows // LANES):
        shift_ref[:, k * LANES : (k + 1) * LANES] = jnp.broadcast_to(
            shift[k : k + 1, :], (8, LANES)
        )
    high, low = halves(x_ref[...])
    xst_ref[...] = jnp.concatenate([high, low, jnp.ones((16, rows), BF16)], 0)

    def peaks(q, unused):
        for r in range(4):
            start = pl.multiple_of((q * 4 + r) * 8, 8)
            z = [
                cross_ref[pl.ds(start, 8), k * LANES : (k + 1) * LANES]
                + shift_ref[:, k * LANES : (k + 1) * LANES]
                for k in range(rows // LANES)
            ]
            top = jnp.max(tree(jnp.maximum, z), 1, keepdims=True)
            peak_ref[pl.ds(start, 8), :] = jnp.broadcast_to(top, (8, LANES))
        return unused

    lax.fori_loop(0, cols // 32, peaks, 0)
    tall = min(256, cols)
    deep = min(1024, rows)

    def block(q, unused):
        span = pl.ds(pl.multiple_of(q * tall, tall), tall)
        acc_ref[...] = jnp.zeros_like(acc_ref)

        def step(c, inner):
            at = pl.multiple_of(c * deep, deep)
            lanes = pl.ds(at, deep)
            highs, lows = [], []
            for k in range(deep // LANES):
                here = pl.ds(at + k * LANES, LANES)
                line = jnp.broadcast_to(shift_ref[0:1, here], (tall, LANES))
                prob = jnp.exp2((cross_ref[span, here] + line) - peak_ref[span, :])
                high, low = halves(prob)
                highs.append(high)
                lows.append(low)
            stack = xst_ref[:, lanes]
            dims_ = (((1,), (1,)), ((), ()))
            acc_ref[...] += lax.dot_general(
                jnp.concatenate(highs, 1), stack, dims_, preferred_element_type=F32
            ) + lax.dot_general(
                jnp.concatenate(lows, 1), stack, dims_, preferred_element_type=F32
            )
            return inner

        lax.fori_loop(0, rows // deep, step, 0)
        acc = acc_ref[...]
        mass = acc[:, 2 * dims : 2 * dims + 1]
        weight = (acc[:, :dims] + acc[:, dims : 2 * dims]) / mass
        weight_ref[:, span] = jnp.concatenate([weight, weight], 1).T[:dims, :]
        mass_ref[span, :] = peak_ref[span, :] + jnp.log2(jnp.broadcast_to(mass, (tall, LANES)))
        return unused

    lax.fori_loop(0, cols // tall, block, 0)
    gather_lanes(lse_ref, mass_ref)


def final_kernel(
    scale, eps_scale, n_parts, x_ref, sl_ref, mask_ref, *refs
):
    ys, gs = refs[:n_parts], refs[n_parts : 2 * n_parts]
    out_ref, xop_ref, yop_ref, yst_ref, shift_ref, cross_ref, peak_ref, acc_ref = refs[2 * n_parts :]
    dims, own = x_ref.shape
    clusters = mask_ref.shape[0]
    cols = gs[0].shape[0] * gs[0].shape[1]
    total = cols * n_parts
    high, low = halves(x_ref[...])
    barred = barred_by(mask_ref, onehot(sl_ref[...], clusters), True)
    stacked = jnp.concatenate([high.astype(F32), low.astype(F32), high.astype(F32), barred], 0)
    xop_ref[...] = stacked.T.astype(BF16)
    for n in range(n_parts):
        at = slice(n * cols, (n + 1) * cols)
        y = ys[n][0:dims, :]
        labels = ys[n][dims : dims + 1, :].astype(jnp.int32)
        high, low = halves(y)
        yst_ref[:, at] = jnp.concatenate([high, low, jnp.ones((16, cols), BF16)], 0)
        high, low = halves(y * scale)
        hot = onehot(labels, clusters).astype(BF16)
        yop_ref[:, at] = jnp.concatenate([high, high, low, hot], 0)
        ysq = jnp.sum(y * y, 0, keepdims=True) * eps_scale
        for k in range(cols // LANES):
            lanes = slice(n * cols + k * LANES, n * cols + (k + 1) * LANES)
            line = gs[n][k : k + 1, :] - ysq[:, k * LANES : (k + 1) * LANES]
            shift_ref[:, lanes] = jnp.broadcast_to(line, (8, LANES))
    peak_ref[...] = jnp.full(peak_ref.shape, 2.0 * BARRED, F32)
    width = min(256, total)

    def fill(q, unused):
        at = pl.multiple_of(q * width, width)
        cross = jnp.dot(xop_ref[...], yop_ref[:, pl.ds(at, width)], preferred_element_type=F32)
        peak = peak_ref[...]
        for p in range(width // LANES):
            here = pl.ds(at + p * LANES, LANES)
            z = cross[:, p * LANES : (p + 1) * LANES] + jnp.broadcast_to(
                shift_ref[0:1, here], (own, LANES)
            )
            cross_ref[:, here] = z
            peak = jnp.maximum(peak, z)
        peak_ref[...] = peak
        return unused

    lax.fori_loop(0, total // width, fill, 0)
    peak_ref[...] = jnp.broadcast_to(jnp.max(peak_ref[...], 1, keepdims=True), peak_ref.shape)
    deep = min(1024, total)
    tall = min(256, own)
    for b in range(own // tall):
        span = slice(b * tall, (b + 1) * tall)
        acc_ref[...] = jnp.zeros_like(acc_ref)

        def step(c, inner):
            at = pl.multiple_of(c * deep, deep)
            highs, lows = [], []
            for k in range(deep // LANES):
                here = pl.ds(at + k * LANES, LANES)
                prob = jnp.exp2(cross_ref[span, here] - peak_ref[span, :])
                high, low = halves(prob)
                highs.append(high)
                lows.append(low)
            stack = yst_ref[:, pl.ds(at, deep)]
            dims_ = (((1,), (1,)), ((), ()))
            acc_ref[...] += lax.dot_general(
                jnp.concatenate(highs, 1), stack, dims_, preferred_element_type=F32
            ) + lax.dot_general(
                jnp.concatenate(lows, 1), stack, dims_, preferred_element_type=F32
            )
            return inner

        lax.fori_loop(0, total // deep, step, 0)
        acc = acc_ref[...]
        mass = acc[:, 2 * dims : 2 * dims + 1]
        weight = (acc[:, :dims] + acc[:, dims : 2 * dims]) / mass
        out_ref[:, span] = jnp.concatenate([weight, weight], 1).T[:dims, :]


def pairs(size, step):
    return [(k, k ^ step) for k in range(size)]


def swap(value, axis, step):
    return lax.ppermute(value, axis, pairs(lax.axis_size(axis), step))


def params(mib):
    return pltpu.CompilerParams(vmem_limit_bytes=mib << 20)


def in_vmem(value):
    return pltpu.with_memory_space_constraint(value, pltpu.VMEM)


def shards(source_pca, target_pca, source_labels, target_labels, block_mask):
    dims, rows = source_pca.shape
    cols = target_pca.shape[1]
    nsrc, ntgt = lax.axis_size("src"), lax.axis_size("tgt")
    total_rows, total_cols = rows * nsrc, cols * ntgt
    kappa = LOG2E / EPSILON
    scale, eps_scale = 2.0 * kappa / dims, kappa / dims
    xl, yl = source_labels.reshape(1, rows), target_labels.reshape(1, cols)
    row_lines, col_lines = (rows // LANES, LANES), (cols // LANES, LANES)
    depth = 3 * dims + block_mask.shape[0]
    sds = jax.ShapeDtypeStruct

    packed = jnp.concatenate([target_pca, yl.astype(F32), jnp.zeros((7, cols), F32)], 0)
    ys = [packed] + [swap(packed, "tgt", k) for k in range(2, ntgt, 2)]
    stacked = jnp.stack(ys)
    other = swap(stacked, "tgt", 1)
    ys = ys + [other[k] for k in range(ntgt // 2)]

    cross, lse, xsq = pl.pallas_call(
        functools.partial(first_kernel, scale, eps_scale),
        out_shape=(pltpu.VMEM((cols, rows), F32), sds(row_lines, F32), sds(row_lines, F32)),
        out_specs=(VMEM,) * 3,
        in_specs=[VMEM] * 5,
        scratch_shapes=[
            pltpu.VMEM((depth, min(256, rows)), BF16),
            pltpu.VMEM((cols, depth), BF16),
            pltpu.VMEM((cols, LANES), F32),
            pltpu.VMEM((cols, LANES), F32),
        ],
        compiler_params=params(12),
        name="first",
    )(source_pca, target_pca, xl, yl, block_mask)

    def rows_parts(lse):
        both = merge([lse, swap(lse, "tgt", 1)])
        return [both] + [swap(both, "tgt", k) for k in range(2, ntgt, 2)]

    def cols_parts(lse):
        return [lse] + [swap(lse, "src", k) for k in range(1, nsrc)]

    for step in range(ITERS):
        parts = rows_parts(lse)
        if step < ITERS - 1:
            col_lse = pl.pallas_call(
                functools.partial(col_kernel, total_rows, len(parts)),
                out_shape=sds(col_lines, F32),
                out_specs=VMEM,
                in_specs=[VMEM] * (2 + len(parts)),
                scratch_shapes=[pltpu.VMEM((8, rows), F32), pltpu.VMEM((cols, LANES), F32)],
                compiler_params=params(8),
                name="col",
            )(in_vmem(cross), xsq, *parts)
            parts = cols_parts(col_lse)
            lse = pl.pallas_call(
                functools.partial(row_kernel, total_cols, len(parts)),
                out_shape=sds(row_lines, F32),
                out_specs=VMEM,
                in_specs=[VMEM] * (1 + len(parts)),
                scratch_shapes=[pltpu.VMEM((cols, LANES), F32)],
                compiler_params=params(8),
                name="row",
            )(in_vmem(cross), *parts)
        else:
            col_lse, weight = pl.pallas_call(
                functools.partial(last_col_kernel, total_rows, len(parts)),
                out_shape=(sds(col_lines, F32), sds((dims, cols), F32)),
                out_specs=(VMEM, VMEM),
                in_specs=[VMEM] * (3 + len(parts)),
                scratch_shapes=[
                    pltpu.VMEM((8, rows), F32),
                    pltpu.VMEM((cols, LANES), F32),
                    pltpu.VMEM((cols, LANES), F32),
                    pltpu.VMEM((2 * dims + 16, rows), BF16),
                    pltpu.VMEM((min(256, cols), 2 * dims + 16), F32),
                ],
                compiler_params=params(16),
                name="last_col",
            )(in_vmem(cross), xsq, source_pca, *parts)
            parts = cols_parts(col_lse)
    col_all = merge(parts)
    pot = -math.log2(total_cols) - col_all
    weights = [weight] + [swap(weight, "src", k) for k in range(1, nsrc)]
    target_projection = sum(
        jnp.exp2(part - col_all).reshape(1, cols) * w for part, w in zip(parts, weights)
    )

    both = jnp.stack([pot, swap(pot, "tgt", 1)])
    gathered = [both] + [swap(both, "tgt", k) for k in range(2, ntgt, 2)]
    gs = [part[0] for part in gathered] + [part[1] for part in gathered]

    own = rows // ntgt
    start = lax.axis_index("tgt") * own
    own_x = lax.dynamic_slice_in_dim(source_pca, start, own, 1)
    own_l = lax.dynamic_slice_in_dim(xl, start, own, 1)
    source_projection = pl.pallas_call(
        functools.partial(final_kernel, scale, eps_scale, ntgt),
        out_shape=sds((dims, own), F32),
        out_specs=VMEM,
        in_specs=[VMEM] * (3 + 2 * ntgt),
        scratch_shapes=[
            pltpu.VMEM((own, depth), BF16),
            pltpu.VMEM((depth, total_cols), BF16),
            pltpu.VMEM((2 * dims + 16, total_cols), BF16),
            pltpu.VMEM((8, total_cols), F32),
            pltpu.VMEM((own, total_cols), F32),
            pltpu.VMEM((own, LANES), F32),
            pltpu.VMEM((min(256, own), 2 * dims + 16), F32),
        ],
        compiler_params=params(44),
        name="final",
    )(own_x, own_l, block_mask, *ys, *gs)
    return (source_projection, target_projection)


def solution(mesh):
    placed = (P(None, "src"), P(None, "tgt"), P("src"), P("tgt"), P())
    return jax.shard_map(
        shards,
        mesh=mesh,
        in_specs=placed,
        out_specs=(P(None, ("src", "tgt")), P(None, "tgt")),
        check_vma=False,
    )
```

```python
import functools
import math

import jax
import jax.numpy as jnp
from jax import lax
from jax.experimental import pallas as pl
from jax.experimental.pallas import tpu as pltpu
from jax.sharding import PartitionSpec as P

EPSILON = 0.05
BARRED = -(2.0**100)
LANES = 128
LOG2E = math.log2(math.e)
F32 = jnp.float32
BF16 = jnp.bfloat16
VMEM = pl.BlockSpec(memory_space=pltpu.VMEM)
HBM = pl.BlockSpec(memory_space=pltpu.HBM)


def halves(value):
    high = value.astype(BF16)
    low = (value - high.astype(F32)).astype(BF16)
    return high, low


def onehot(labels, clusters):
    series = lax.broadcasted_iota(jnp.int32, (clusters, labels.shape[1]), 0)
    return series == labels


def barred_by(mask_ref, hot, transposed):
    stop = (1.0 - mask_ref[...].astype(F32)).astype(BF16)
    dims = (((0,), (0,)), ((), ())) if transposed else (((1,), (0,)), ((), ()))
    picked = lax.dot_general(stop, hot.astype(BF16), dims, preferred_element_type=F32)
    return picked * BARRED


def tree(combine, parts):
    parts = list(parts)
    while len(parts) > 1:
        parts = [
            combine(parts[k], parts[k + 1]) if k + 1 < len(parts) else parts[k]
            for k in range(0, len(parts), 2)
        ]
    return parts[0]


def merge(tops):
    peak = tree(jnp.maximum, tops)
    return peak + jnp.log2(tree(jnp.add, [jnp.exp2(part - peak) for part in tops]))


def spread_lanes(dst_ref, rows):
    for k in range(rows.shape[0]):
        square = jnp.broadcast_to(rows[k : k + 1, :], (LANES, LANES))
        dst_ref[k * LANES : (k + 1) * LANES, :] = square.T


def gather_lanes(dst_ref, column_ref):
    for k in range(dst_ref.shape[0]):
        dst_ref[k : k + 1, :] = column_ref[k * LANES : (k + 1) * LANES, :].T[0:1, :]


def online(peak, total, z):
    newer = jnp.maximum(peak, tree(jnp.maximum, z))
    fresh = tree(jnp.add, [jnp.exp2(part - newer) for part in z])
    return newer, total * jnp.exp2(peak - newer) + fresh


def down(peak, total):
    top = jnp.max(peak, 0, keepdims=True)
    return top + jnp.log2(jnp.sum(total * jnp.exp2(peak - top), 0, keepdims=True))


def fetch(pairs, sems):
    copies = [pltpu.make_async_copy(src, dst, sems.at[k]) for k, (src, dst) in enumerate(pairs)]
    for copy in copies:
        copy.start()
    return copies


def first_kernel(
    scale, eps_scale, x_hbm, y_hbm, sl_hbm, tl_hbm, mask_hbm,
    cross_ref, lse_ref, xsq_ref,
    x_ref, y_ref, sl_ref, tl_ref, mask_ref, yop_ref, ysq_ref, sems,
):
    copies = fetch(
        [(y_hbm, y_ref), (tl_hbm, tl_ref), (mask_hbm, mask_ref), (sl_hbm, sl_ref), (x_hbm, x_ref)],
        sems,
    )
    _, rows = x_ref.shape
    cols = y_ref.shape[1]
    clusters = mask_ref.shape[0]
    for copy in copies[:3]:
        copy.wait()
    high, low = halves(y_ref[...] * scale)
    barred = barred_by(mask_ref, onehot(tl_ref[...], clusters), False)
    stacked = jnp.concatenate([high.astype(F32), high.astype(F32), low.astype(F32), barred], 0)
    yop_ref[...] = stacked.T.astype(BF16)
    ysq = jnp.sum(y_ref[...] * y_ref[...], 0, keepdims=True) * (-eps_scale)
    for k in range(cols // LANES):
        square = jnp.broadcast_to(ysq[:, k * LANES : (k + 1) * LANES], (LANES, LANES))
        ysq_ref[k * LANES : (k + 1) * LANES, :] = square.T
    for copy in copies[3:]:
        copy.wait()
    width = min(512, rows)
    narrow = min(256, width)
    depth = min(64, cols)
    base = rows // LANES
    for k in range(cols // LANES):
        lse_ref[base + k : base + k + 1, :] = tl_ref[:, k * LANES : (k + 1) * LANES].astype(F32)

    def chunk(q, unused):
        for half in range(width // narrow):
            line = q * (width // LANES) + half * (narrow // LANES)
            start = pl.multiple_of(q * width + half * narrow, narrow)
            x = x_ref[:, pl.ds(start, narrow)]
            high, low = halves(x)
            hot = onehot(sl_ref[:, pl.ds(start, narrow)], clusters).astype(BF16)
            xop = jnp.concatenate([high, low, high, hot], 0)
            xsq = jnp.sum(x * x, 0, keepdims=True) * eps_scale
            cross = jnp.dot(yop_ref[...], xop, preferred_element_type=F32)
            per = narrow // LANES
            peaks = [jnp.full((8, LANES), 2.0 * BARRED, F32)] * per
            totals = [jnp.zeros((8, LANES), F32)] * per
            for top in range(0, cols, depth):
                for p in range(per):
                    here = pl.ds(pl.multiple_of(start + p * LANES, LANES), LANES)
                    z = []
                    for r in range(top, top + depth, 8):
                        z.append(cross[r : r + 8, p * LANES : (p + 1) * LANES] + ysq_ref[r : r + 8, :])
                        cross_ref[r : r + 8, here] = z[-1]
                    peaks[p], totals[p] = online(peaks[p], totals[p], z)
            for p in range(per):
                xsq_ref[pl.ds(line + p, 1), :] = xsq[:, p * LANES : (p + 1) * LANES]
                lse_ref[pl.ds(line + p, 1), :] = down(peaks[p], totals[p])
        return unused

    lax.fori_loop(0, rows // width, chunk, 0)


def source_shift(parts_refs, xsq_ref, total_rows):
    lines = xsq_ref.shape[0]
    lse = merge([ref[0:lines, :] for ref in parts_refs]) - xsq_ref[...]
    pot = -math.log2(total_rows) - lse
    return pot - xsq_ref[...]


def target_potential(parts_refs, total_cols):
    return -math.log2(total_cols) - merge([ref[...] for ref in parts_refs])


def spread_rows(shift_ref, shift):
    for k in range(shift.shape[0]):
        shift_ref[:, k * LANES : (k + 1) * LANES] = jnp.broadcast_to(shift[k : k + 1, :], (8, LANES))


def col_kernel(total_rows, n_parts, cross_ref, xsq_ref, *refs):
    parts, (lse_ref, pot_ref, shift_ref, peak_ref, mass_ref) = refs[:n_parts], refs[n_parts:]
    cols, rows = cross_ref.shape
    pot_ref[...] = source_shift(parts, xsq_ref, total_rows)
    spread_rows(shift_ref, pot_ref[...])
    deep = min(16, rows // LANES)
    groups = 8

    def block(q, unused):
        for r in range(groups):
            start = pl.ds(pl.multiple_of((q * groups + r) * 8, 8), 8)
            peak = jnp.full((8, LANES), 2.0 * BARRED, F32)
            total = jnp.zeros((8, LANES), F32)
            for c in range(0, rows // LANES, deep):
                lanes = [slice(k * LANES, (k + 1) * LANES) for k in range(c, c + deep)]
                z = [cross_ref[start, at] + shift_ref[:, at] for at in lanes]
                peak, total = online(peak, total, z)
            peak_ref[start, :] = peak
            mass_ref[start, :] = total
        return unused

    lax.fori_loop(0, cols // 8 // groups, block, 0)
    peak = peak_ref[...]
    top = jnp.max(peak, 1, keepdims=True)
    mass = jnp.sum(mass_ref[...] * jnp.exp2(peak - top), 1, keepdims=True)
    mass_ref[...] = jnp.broadcast_to(top + jnp.log2(mass), mass_ref.shape)
    gather_lanes(lse_ref, mass_ref)


def row_kernel(total_cols, n_parts, cross_ref, pot_ref, *refs):
    parts, (plan_ref, sums_ref, g_ref, shift_ref) = refs[:n_parts], refs[n_parts:]
    g_ref[...] = target_potential(parts, total_cols)
    spread_lanes(shift_ref, g_ref[...])
    cols, rows = plan_ref.shape
    width = min(512, rows)

    def block(q, unused):
        for p in range(width // LANES):
            at = pl.ds(pl.multiple_of(q * width + p * LANES, LANES), LANES)
            line = pl.ds(q * (width // LANES) + p, 1)
            pot = jnp.broadcast_to(pot_ref[line, :], (8, LANES))
            totals = []
            for start in range(0, cols, 64):
                t = []
                for r in range(start, start + 64, 8):
                    t.append(jnp.exp2(plan_ref[r : r + 8, at] + (shift_ref[r : r + 8, :] + pot)))
                    plan_ref[r : r + 8, at] = t[-1]
                totals.append(tree(jnp.add, t))
            sums_ref[line, :] = jnp.sum(tree(jnp.add, totals), 0, keepdims=True)
        return unused

    lax.fori_loop(0, rows // width, block, 0)


def weigh(segments, acc_ref, out_ref, mass_ref, rows, tall):
    dims = out_ref.shape[0]

    def block(q, unused):
        span = pl.ds(pl.multiple_of(q * tall, tall), tall)
        first = True
        for make, stack_ref in segments:
            width = stack_ref.shape[0]
            deep = min(2048, width)
            for c in range(0, width, deep):
                highs, lows = [], []
                for k in range(c, c + deep, LANES):
                    high, low = halves(make(span, k))
                    highs.append(high)
                    lows.append(low)
                lhs = jnp.concatenate([jnp.concatenate(highs, 1), jnp.concatenate(lows, 1)], 0)
                part = jnp.dot(lhs, stack_ref[c : c + deep, :], preferred_element_type=F32)
                part = part[:tall] + part[tall:]
                if first:
                    acc_ref[...] = part
                else:
                    acc_ref[...] += part
                first = False
        acc = acc_ref[...]
        mass = acc[:, 2 * dims : 2 * dims + 1]
        weight = acc[:, :dims] + acc[:, dims : 2 * dims]
        if mass_ref is None:
            weight = weight / mass
        else:
            mass_ref[span, :] = jnp.broadcast_to(mass, (tall, LANES))
        out_ref[:, span] = jnp.concatenate([weight, weight], 1).T[:dims, :]
        return unused

    lax.fori_loop(0, rows // tall, block, 0)


def stack_columns(stack_ref, at, high, low):
    dims, n = high.shape
    both = jnp.concatenate([high.astype(F32), low.astype(F32)], 0)
    stack_ref[at, : 2 * dims] = both.T.astype(BF16)
    column = lax.broadcasted_iota(jnp.int32, (n, 16), 1)
    stack_ref[at, 2 * dims :] = jnp.where(column < 8, 1.0, 0.0).astype(BF16)


def stack_kernel(scale, x_hbm, sl_hbm, mask_ref, xst_ref, xop_ref, x_ref, own_ref, sl_ref, sems):
    own, rows = xop_ref.shape[0], x_ref.shape[1]
    start = pl.multiple_of(lax.axis_index("tgt") * own, own)
    mine = pl.ds(start, own)
    copies = fetch(
        [(x_hbm.at[:, mine], own_ref), (sl_hbm.at[:, mine], sl_ref), (x_hbm, x_ref)], sems
    )
    clusters = mask_ref.shape[0]
    for copy in copies[:2]:
        copy.wait()
    high, low = halves(own_ref[...] * scale)
    barred = barred_by(mask_ref, onehot(sl_ref[...], clusters), True)
    stacked = jnp.concatenate([high.astype(F32), low.astype(F32), high.astype(F32), barred], 0)
    xop_ref[...] = stacked.T.astype(BF16)
    copies[2].wait()
    step = min(512, rows)
    for k in range(0, rows, step):
        stack_columns(xst_ref, slice(k, k + step), *halves(x_ref[:, k : k + step]))


def last_col_kernel(total_rows, n_parts, plan_ref, xst_ref, *refs):
    parts = refs[:n_parts]
    sums_ref, weight_ref, scale_ref, mass_ref, acc_ref = refs[n_parts:]
    cols = plan_ref.shape[0]
    tall = acc_ref.shape[0]
    spread_rows(scale_ref, 1.0 / (total_rows * tree(jnp.add, [ref[...] for ref in parts])))

    def make(span, k):
        line = jnp.broadcast_to(scale_ref[0:1, k : k + LANES], (tall, LANES))
        return plan_ref[span, k : k + LANES] * line

    weigh([(make, xst_ref)], acc_ref, weight_ref, mass_ref, cols, tall)
    gather_lanes(sums_ref, mass_ref)


def ready_kernel(eps_scale, n_near, lines, xop_ref, pot_ref, *refs):
    near, far, labels = refs[:n_near], refs[n_near : 2 * n_near], refs[2 * n_near : 3 * n_near]
    cross_ref, yst_ref, yop_ref, ysq_ref, shift_ref = refs[3 * n_near :]
    own, total = cross_ref.shape
    dims, cols = near[0].shape
    clusters = yop_ref.shape[0] - 3 * dims
    tiles = cols // LANES
    place = lax.axis_index("tgt")
    spread_lanes(shift_ref, pot_ref[pl.ds(place * (own // LANES), own // LANES), :])
    for n, ref in enumerate(near + far):
        at = slice(n * cols, (n + 1) * cols)
        y = ref[...]
        high, low = halves(y)
        stack_columns(yst_ref, at, high, low)
        yop_ref[: 3 * dims, at] = jnp.concatenate([high, high, low], 0)
        side, which = divmod(n, n_near)
        for k in range(tiles):
            line = lines + side * tiles + k
            lanes = slice(n * cols + k * LANES, n * cols + (k + 1) * LANES)
            label = labels[which][line : line + 1, :].astype(jnp.int32)
            yop_ref[3 * dims :, lanes] = onehot(label, clusters).astype(BF16)
        ysq = jnp.sum(y * y, 0, keepdims=True) * (-eps_scale)
        ysq_ref[:, at] = jnp.broadcast_to(ysq, (8, cols))
    width = min(512, total)

    def fill(q, unused):
        at = pl.multiple_of(q * width, width)
        cross = jnp.dot(xop_ref[...], yop_ref[:, pl.ds(at, width)], preferred_element_type=F32)
        for p in range(width // LANES):
            here = pl.ds(at + p * LANES, LANES)
            line = jnp.broadcast_to(ysq_ref[0:1, here], (own, LANES))
            cross_ref[:, here] = cross[:, p * LANES : (p + 1) * LANES] + (shift_ref[...] + line)
        return unused

    lax.fori_loop(0, total // width, fill, 0)


def final_kernel(sizes, *refs):
    n = len(sizes)
    crosses, stacks, gs = refs[:n], refs[n : 2 * n], refs[2 * n : -3]
    out_ref, shift_ref, acc_ref = refs[-3:]
    tall = acc_ref.shape[0]
    segments = []
    col = first = 0
    for size, cross_ref, stack_ref in zip(sizes, crosses, stacks):
        base = col
        for side in range(2):
            for g in gs[first : first + size]:
                for k in range(g.shape[1]):
                    shift_ref[:, col : col + LANES] = jnp.broadcast_to(
                        g[side, k : k + 1, :], (8, LANES)
                    )
                    col += LANES
        first += size

        def make(span, k, cross_ref=cross_ref, base=base):
            line = jnp.broadcast_to(shift_ref[0:1, base + k : base + k + LANES], (tall, LANES))
            return jnp.exp2(cross_ref[span, k : k + LANES] + line)

        segments.append((make, stack_ref))
    weigh(segments, acc_ref, out_ref, None, crosses[0].shape[0], tall)


def pairs(size, step):
    return [(k, k ^ step) for k in range(size)]


def swap(value, axis, step):
    return lax.ppermute(value, axis, pairs(lax.axis_size(axis), step))


def params(mib):
    return pltpu.CompilerParams(vmem_limit_bytes=mib << 20)


def in_vmem(value):
    return pltpu.with_memory_space_constraint(value, pltpu.VMEM)


def in_hbm(value):
    return pltpu.with_memory_space_constraint(value, pltpu.HBM)


def shards(source_pca, target_pca, source_labels, target_labels, block_mask):
    dims, rows = source_pca.shape
    cols = target_pca.shape[1]
    nsrc, ntgt = lax.axis_size("src"), lax.axis_size("tgt")
    total_rows, total_cols = rows * nsrc, cols * ntgt
    kappa = LOG2E / EPSILON
    scale, eps_scale = 2.0 * kappa / dims, kappa / dims
    xl, yl = source_labels.reshape(1, rows), target_labels.reshape(1, cols)
    row_lines, col_lines = (rows // LANES, LANES), (cols // LANES, LANES)
    depth = 3 * dims + block_mask.shape[0]
    sds = jax.ShapeDtypeStruct

    steps = list(range(2, ntgt, 2))
    third = max(1, len(steps) // 3)
    legs = [[0], steps[:third], steps[third : 2 * third], steps[2 * third :]]
    near, far = [], []
    for ks in legs:
        near.append([swap(target_pca, "tgt", k) if k else target_pca for k in ks])
        far.append([swap(y, "tgt", 1) for y in near[-1]])

    cross, lse, xsq = pl.pallas_call(
        functools.partial(first_kernel, scale, eps_scale),
        out_shape=(
            pltpu.VMEM((cols, rows), F32),
            sds((row_lines[0] + col_lines[0], LANES), F32),
            sds(row_lines, F32),
        ),
        out_specs=(VMEM,) * 3,
        in_specs=[HBM] * 5,
        scratch_shapes=[
            pltpu.VMEM((dims, rows), F32),
            pltpu.VMEM((dims, cols), F32),
            pltpu.VMEM((1, rows), jnp.int32),
            pltpu.VMEM((1, cols), jnp.int32),
            pltpu.VMEM(block_mask.shape, jnp.int32),
            pltpu.VMEM((cols, depth), BF16),
            pltpu.VMEM((cols, LANES), F32),
            pltpu.SemaphoreType.DMA((5,)),
        ],
        compiler_params=params(12),
        name="first",
    )(*map(in_hbm, (source_pca, target_pca, xl, yl, block_mask)))

    own = rows // ntgt
    xst, xop = pl.pallas_call(
        functools.partial(stack_kernel, scale),
        out_shape=(sds((rows, 2 * dims + 16), BF16), sds((own, depth), BF16)),
        out_specs=(VMEM, VMEM),
        in_specs=[HBM, HBM, VMEM],
        scratch_shapes=[
            pltpu.VMEM((dims, rows), F32),
            pltpu.VMEM((dims, own), F32),
            pltpu.VMEM((1, own), jnp.int32),
            pltpu.SemaphoreType.DMA((3,)),
        ],
        compiler_params=params(8),
        name="stack",
    )(in_hbm(source_pca), in_hbm(xl), block_mask)

    def rows_parts(value, combine):
        other = swap(value, "tgt", 1)
        lines = row_lines[0]
        both = combine([value[:lines], other[:lines]])
        if value.shape[0] > lines:
            both = jnp.concatenate([both, value[lines:], other[lines:]], 0)
        return {0: both} | {k: swap(both, "tgt", k) for k in steps}

    def cols_parts(value):
        return [value] + [swap(value, "src", k) for k in range(1, nsrc)]

    add = functools.partial(tree, jnp.add)
    labelled = rows_parts(lse, merge)
    parts = list(labelled.values())
    col_lse, pots = pl.pallas_call(
        functools.partial(col_kernel, total_rows, len(parts)),
        out_shape=(sds(col_lines, F32), sds(row_lines, F32)),
        out_specs=(VMEM, VMEM),
        in_specs=[VMEM] * (2 + len(parts)),
        scratch_shapes=[
            pltpu.VMEM((8, rows), F32),
            pltpu.VMEM((cols, LANES), F32),
            pltpu.VMEM((cols, LANES), F32),
        ],
        compiler_params=params(8),
        name="col",
    )(in_vmem(cross), xsq, *parts)
    parts = cols_parts(col_lse)
    plan, sums, g = pl.pallas_call(
        functools.partial(row_kernel, total_cols, len(parts)),
        out_shape=(pltpu.VMEM((cols, rows), F32), sds(row_lines, F32), sds(col_lines, F32)),
        out_specs=(VMEM,) * 3,
        in_specs=[VMEM] * (2 + len(parts)),
        scratch_shapes=[pltpu.VMEM((cols, LANES), F32)],
        input_output_aliases={0: 0},
        compiler_params=params(8),
        name="row",
    )(in_vmem(cross), pots, *parts)
    parts = list(rows_parts(sums, add).values())
    mass, weight = pl.pallas_call(
        functools.partial(last_col_kernel, total_rows, len(parts)),
        out_shape=(sds(col_lines, F32), sds((dims, cols), F32)),
        out_specs=(VMEM, VMEM),
        in_specs=[VMEM] * (2 + len(parts)),
        scratch_shapes=[
            pltpu.VMEM((8, rows), F32),
            pltpu.VMEM((cols, LANES), F32),
            pltpu.VMEM((min(256, cols), 2 * dims + 16), F32),
        ],
        compiler_params=params(8),
        name="last_col",
    )(in_vmem(plan), xst, *parts)
    mass = add(cols_parts(mass))
    weights = [weight] + [swap(weight, "src", k) for k in range(1, nsrc)]
    pot = g - math.log2(total_cols) - jnp.log2(mass)

    crosses, stacks, sizes = [], [], [len(ks) for ks in legs]
    for leg, ks in enumerate(legs):
        width = 2 * len(ks) * cols
        own_cross, stack = pl.pallas_call(
            functools.partial(ready_kernel, eps_scale, len(ks), row_lines[0]),
            out_shape=(pltpu.VMEM((own, width), F32), sds((width, 2 * dims + 16), BF16)),
            out_specs=(VMEM, VMEM),
            in_specs=[VMEM] * (2 + 3 * len(ks)),
            scratch_shapes=[
                pltpu.VMEM((depth, width), BF16),
                pltpu.VMEM((8, width), F32),
                pltpu.VMEM((own, LANES), F32),
            ],
            compiler_params=params(4 + (width * (2 * depth + 32) >> 20)),
            name="ready",
        )(xop, pots, *near[leg], *far[leg], *[labelled[k] for k in ks])
        crosses.append(in_vmem(own_cross))
        stacks.append(stack)

    both = jnp.stack([pot, swap(pot, "tgt", 1)])
    gs = [both] + [swap(both, "tgt", k) for k in range(2, ntgt, 2)]
    source_projection = pl.pallas_call(
        functools.partial(final_kernel, sizes),
        out_shape=sds((dims, own), F32),
        out_specs=VMEM,
        in_specs=[VMEM] * (2 * len(sizes) + len(gs)),
        scratch_shapes=[
            pltpu.VMEM((8, total_cols), F32),
            pltpu.VMEM((min(256, own), 2 * dims + 16), F32),
        ],
        compiler_params=params(8),
        name="final",
    )(*crosses, *stacks, *gs)
    target_projection = add(weights) / mass.reshape(1, cols)
    return (source_projection, target_projection)


def solution(mesh):
    placed = (P(None, "src"), P(None, "tgt"), P("src"), P("tgt"), P())
    return jax.shard_map(
        shards,
        mesh=mesh,
        in_specs=placed,
        out_specs=(P(None, ("src", "tgt")), P(None, "tgt")),
        check_vma=False,
    )
```

```python
import functools
import math

import jax
import jax.numpy as jnp
from jax import lax
from jax.experimental import pallas as pl
from jax.experimental.pallas import tpu as pltpu
from jax.sharding import PartitionSpec as P

EPSILON = 0.05
BARRED = -(2.0**100)
LANES = 128
LOG2E = math.log2(math.e)
F32 = jnp.float32
BF16 = jnp.bfloat16
VMEM = pl.BlockSpec(memory_space=pltpu.VMEM)
HBM = pl.BlockSpec(memory_space=pltpu.HBM)


def halves(value):
    high = value.astype(BF16)
    low = (value - high.astype(F32)).astype(BF16)
    return high, low


def onehot(labels, clusters):
    series = lax.broadcasted_iota(jnp.int32, (clusters, labels.shape[1]), 0)
    return series == labels


def barred_by(mask_ref, hot, transposed):
    stop = (1.0 - mask_ref[...].astype(F32)).astype(BF16)
    dims = (((0,), (0,)), ((), ())) if transposed else (((1,), (0,)), ((), ()))
    picked = lax.dot_general(stop, hot.astype(BF16), dims, preferred_element_type=F32)
    return picked * BARRED


def tree(combine, parts):
    parts = list(parts)
    while len(parts) > 1:
        parts = [
            combine(parts[k], parts[k + 1]) if k + 1 < len(parts) else parts[k]
            for k in range(0, len(parts), 2)
        ]
    return parts[0]


def merge(tops):
    peak = tree(jnp.maximum, tops)
    return peak + jnp.log2(tree(jnp.add, [jnp.exp2(part - peak) for part in tops]))


def spread_lanes(dst_ref, rows):
    for k in range(rows.shape[0]):
        square = jnp.broadcast_to(rows[k : k + 1, :], (LANES, LANES))
        dst_ref[k * LANES : (k + 1) * LANES, :] = square.T


def gather_lanes(dst_ref, column_ref):
    for k in range(dst_ref.shape[0]):
        dst_ref[k : k + 1, :] = column_ref[k * LANES : (k + 1) * LANES, :].T[0:1, :]


def online(peak, total, z):
    newer = jnp.maximum(peak, tree(jnp.maximum, z))
    fresh = tree(jnp.add, [jnp.exp2(part - newer) for part in z])
    return newer, total * jnp.exp2(peak - newer) + fresh


def down(peak, total):
    top = jnp.max(peak, 0, keepdims=True)
    return top + jnp.log2(jnp.sum(total * jnp.exp2(peak - top), 0, keepdims=True))


def fetch(pairs, sems):
    copies = [pltpu.make_async_copy(src, dst, sems.at[k]) for k, (src, dst) in enumerate(pairs)]
    for copy in copies:
        copy.start()
    return copies


def first_kernel(
    scale, eps_scale, x_hbm, y_hbm, sl_hbm, tl_hbm, mask_hbm,
    cross_ref, lse_ref, xsq_ref,
    x_ref, y_ref, sl_ref, tl_ref, mask_ref, yop_ref, ysq_ref, sems,
):
    copies = fetch(
        [(y_hbm, y_ref), (tl_hbm, tl_ref), (mask_hbm, mask_ref), (sl_hbm, sl_ref), (x_hbm, x_ref)],
        sems,
    )
    _, rows = x_ref.shape
    cols = y_ref.shape[1]
    clusters = mask_ref.shape[0]
    for copy in copies[:3]:
        copy.wait()
    high, low = halves(y_ref[...] * scale)
    barred = barred_by(mask_ref, onehot(tl_ref[...], clusters), False)
    stacked = jnp.concatenate([high.astype(F32), high.astype(F32), low.astype(F32), barred], 0)
    yop_ref[...] = stacked.T.astype(BF16)
    ysq = jnp.sum(y_ref[...] * y_ref[...], 0, keepdims=True) * (-eps_scale)
    for k in range(cols // LANES):
        square = jnp.broadcast_to(ysq[:, k * LANES : (k + 1) * LANES], (LANES, LANES))
        ysq_ref[k * LANES : (k + 1) * LANES, :] = square.T
    for copy in copies[3:]:
        copy.wait()
    width = min(1024, rows)
    narrow = min(256, width)
    depth = min(32, cols)
    base = rows // LANES
    for k in range(cols // LANES):
        lse_ref[base + k : base + k + 1, :] = tl_ref[:, k * LANES : (k + 1) * LANES].astype(F32)

    def chunk(q, unused):
        base = pl.multiple_of(q * width, width)
        here = cross_ref.at[:, pl.ds(base, width)]
        xs = x_ref.at[:, pl.ds(base, width)]
        labels = sl_ref.at[:, pl.ds(base, width)]
        per = narrow // LANES
        for n in range(0, width, narrow):
            x = xs[:, n : n + narrow]
            high, low = halves(x)
            hot = onehot(labels[:, n : n + narrow], clusters).astype(BF16)
            xop = jnp.concatenate([high, low, high, hot], 0)
            xsq = jnp.sum(x * x, 0, keepdims=True) * eps_scale
            cross = jnp.dot(yop_ref[...], xop, preferred_element_type=F32)
            peaks = [jnp.full((8, LANES), 2.0 * BARRED, F32)] * per
            totals = [jnp.zeros((8, LANES), F32)] * per
            for top in range(0, cols, depth):
                for p in range(per):
                    z = []
                    for r in range(top, top + depth, 8):
                        z.append(cross[r : r + 8, p * LANES : (p + 1) * LANES] + ysq_ref[r : r + 8, :])
                        here[r : r + 8, n + p * LANES : n + (p + 1) * LANES] = z[-1]
                    peaks[p], totals[p] = online(peaks[p], totals[p], z)
            for p in range(per):
                line = pl.ds(q * (width // LANES) + n // LANES + p, 1)
                xsq_ref[line, :] = xsq[:, p * LANES : (p + 1) * LANES]
                lse_ref[line, :] = down(peaks[p], totals[p])
        return unused

    lax.fori_loop(0, rows // width, chunk, 0)


def source_shift(parts_refs, xsq_ref, total_rows):
    lines = xsq_ref.shape[0]
    lse = merge([ref[0:lines, :] for ref in parts_refs]) - xsq_ref[...]
    pot = -math.log2(total_rows) - lse
    return pot - xsq_ref[...]


def target_potential(parts_refs, total_cols):
    return -math.log2(total_cols) - merge([ref[...] for ref in parts_refs])


def spread_rows(shift_ref, shift):
    for k in range(shift.shape[0]):
        shift_ref[:, k * LANES : (k + 1) * LANES] = jnp.broadcast_to(shift[k : k + 1, :], (8, LANES))


def col_kernel(total_rows, n_parts, cross_ref, xsq_ref, *refs):
    parts, (lse_ref, pot_ref, shift_ref, peak_ref, mass_ref) = refs[:n_parts], refs[n_parts:]
    cols, rows = cross_ref.shape
    pot_ref[...] = source_shift(parts, xsq_ref, total_rows)
    spread_rows(shift_ref, pot_ref[...])
    deep = min(16, rows // LANES)
    groups = 8

    def block(q, unused):
        for r in range(groups):
            start = pl.ds(pl.multiple_of((q * groups + r) * 8, 8), 8)
            peak = jnp.full((8, LANES), 2.0 * BARRED, F32)
            total = jnp.zeros((8, LANES), F32)
            for c in range(0, rows // LANES, deep):
                lanes = [slice(k * LANES, (k + 1) * LANES) for k in range(c, c + deep)]
                z = [cross_ref[start, at] + shift_ref[:, at] for at in lanes]
                peak, total = online(peak, total, z)
            peak_ref[start, :] = peak
            mass_ref[start, :] = total
        return unused

    lax.fori_loop(0, cols // 8 // groups, block, 0)
    peak = peak_ref[...]
    top = jnp.max(peak, 1, keepdims=True)
    mass = jnp.sum(mass_ref[...] * jnp.exp2(peak - top), 1, keepdims=True)
    mass_ref[...] = jnp.broadcast_to(top + jnp.log2(mass), mass_ref.shape)
    gather_lanes(lse_ref, mass_ref)


def row_kernel(total_cols, n_parts, cross_ref, pot_ref, *refs):
    parts, (plan_ref, sums_ref, g_ref, shift_ref) = refs[:n_parts], refs[n_parts:]
    g_ref[...] = target_potential(parts, total_cols)
    spread_lanes(shift_ref, g_ref[...])
    cols, rows = plan_ref.shape
    width = min(512, rows)

    def block(q, unused):
        tiles = range(width // LANES)
        here = plan_ref.at[:, pl.ds(pl.multiple_of(q * width, width), width)]
        lines = q * (width // LANES)
        pot = [jnp.broadcast_to(pot_ref[pl.ds(lines + p, 1), :], (8, LANES)) for p in tiles]
        totals = [[] for p in tiles]
        for start in range(0, cols, 32):
            t = [[] for p in tiles]
            for r in range(start, start + 32, 8):
                for p in tiles:
                    at = slice(p * LANES, (p + 1) * LANES)
                    part = jnp.exp2(here[r : r + 8, at] + (shift_ref[r : r + 8, :] + pot[p]))
                    here[r : r + 8, at] = part
                    t[p].append(part)
            for p in tiles:
                totals[p] = [tree(jnp.add, totals[p] + t[p])]
        for p in tiles:
            sums_ref[pl.ds(lines + p, 1), :] = jnp.sum(totals[p][0], 0, keepdims=True)
        return unused

    lax.fori_loop(0, rows // width, block, 0)


def weigh(segments, high_ref, low_ref, out_ref, mass_ref, rows):
    dims = out_ref.shape[0]
    tall = high_ref.shape[1]
    short = low_ref.shape[0]
    lanes = (((1,), (1,)), ((), ()))

    def block(q, unused):
        span = pl.ds(pl.multiple_of(q * tall, tall), tall)
        first = True
        for make, stack_ref in segments:
            width = stack_ref.shape[1]
            deep = min(1024, width)
            for c in range(0, width, deep):
                highs, lows = [], []
                for k in range(c, c + deep, LANES):
                    high, low = halves(make(span, k))
                    highs.append(high)
                    lows.append(low)
                stack = stack_ref[:, c : c + deep]
                with_high = lax.dot_general(
                    stack, jnp.concatenate(highs, 1), lanes, preferred_element_type=F32
                )
                with_low = lax.dot_general(
                    stack[:short], jnp.concatenate(lows, 1), lanes, preferred_element_type=F32
                )
                if first:
                    high_ref[...] = with_high
                    low_ref[...] = with_low
                else:
                    high_ref[...] += with_high
                    low_ref[...] += with_low
                first = False
        mass = high_ref[dims : dims + 1, :] + low_ref[dims : dims + 1, :]
        weight = (high_ref[:dims, :] + low_ref[:dims, :]) + high_ref[short:, :]
        if mass_ref is None:
            weight = weight / mass
        else:
            for k in range(tall // LANES):
                line = pl.ds(q * (tall // LANES) + k, 1)
                mass_ref[line, :] = mass[:, k * LANES : (k + 1) * LANES]
        out_ref[:, span] = weight
        return unused

    lax.fori_loop(0, rows // tall, block, 0)


def stack_lines(stack_ref, at, high, low):
    _, n = high.shape
    stack_ref[:, at] = jnp.concatenate([high, jnp.ones((16, n), BF16), low], 0)


def stack_kernel(
    scale, x_hbm, sl_hbm, mask_hbm, xst_ref, xop_ref, x_ref, own_ref, sl_ref, mask_ref, sems
):
    own, rows = xop_ref.shape[0], x_ref.shape[1]
    start = pl.multiple_of(lax.axis_index("tgt") * own, own)
    mine = pl.ds(start, own)
    copies = fetch(
        [
            (x_hbm.at[:, mine], own_ref),
            (sl_hbm.at[:, mine], sl_ref),
            (mask_hbm, mask_ref),
            (x_hbm, x_ref),
        ],
        sems,
    )
    clusters = mask_ref.shape[0]
    for copy in copies[:3]:
        copy.wait()
    high, low = halves(own_ref[...] * scale)
    barred = barred_by(mask_ref, onehot(sl_ref[...], clusters), True)
    stacked = jnp.concatenate([high.astype(F32), low.astype(F32), high.astype(F32), barred], 0)
    xop_ref[...] = stacked.T.astype(BF16)
    copies[3].wait()
    step = min(512, rows)
    for k in range(0, rows, step):
        stack_lines(xst_ref, slice(k, k + step), *halves(x_ref[:, k : k + step]))


def last_col_kernel(total_rows, n_parts, plan_ref, xst_ref, *refs):
    parts = refs[:n_parts]
    sums_ref, weight_ref, scale_ref, high_ref, low_ref = refs[n_parts:]
    cols = plan_ref.shape[0]
    tall = high_ref.shape[1]
    spread_rows(scale_ref, 1.0 / (total_rows * tree(jnp.add, [ref[...] for ref in parts])))

    def make(span, k):
        line = jnp.broadcast_to(scale_ref[0:1, k : k + LANES], (tall, LANES))
        return plan_ref[span, k : k + LANES] * line

    weigh([(make, xst_ref)], high_ref, low_ref, weight_ref, sums_ref, cols)


def ready_kernel(eps_scale, n_near, lines, xop_ref, pot_ref, *refs):
    near, far, labels = refs[:n_near], refs[n_near : 2 * n_near], refs[2 * n_near : 3 * n_near]
    cross_ref, yst_ref, yop_ref, ysq_ref, shift_ref = refs[3 * n_near :]
    own, total = cross_ref.shape
    dims, cols = near[0].shape
    clusters = yop_ref.shape[0] - 3 * dims
    tiles = cols // LANES
    place = lax.axis_index("tgt")
    spread_lanes(shift_ref, pot_ref[pl.ds(place * (own // LANES), own // LANES), :])
    for n, ref in enumerate(near + far):
        at = slice(n * cols, (n + 1) * cols)
        y = ref[...]
        high, low = halves(y)
        stack_lines(yst_ref, at, high, low)
        yop_ref[: 3 * dims, at] = jnp.concatenate([high, high, low], 0)
        side, which = divmod(n, n_near)
        for k in range(tiles):
            line = lines + side * tiles + k
            lanes = slice(n * cols + k * LANES, n * cols + (k + 1) * LANES)
            label = labels[which][line : line + 1, :].astype(jnp.int32)
            yop_ref[3 * dims :, lanes] = onehot(label, clusters).astype(BF16)
        ysq = jnp.sum(y * y, 0, keepdims=True) * (-eps_scale)
        ysq_ref[:, at] = jnp.broadcast_to(ysq, (8, cols))
    width = min(1024, total)

    def fill(q, unused):
        at = pl.multiple_of(q * width, width)
        cross = jnp.dot(xop_ref[...], yop_ref[:, pl.ds(at, width)], preferred_element_type=F32)
        for p in range(width // LANES):
            here = pl.ds(at + p * LANES, LANES)
            line = jnp.broadcast_to(ysq_ref[0:1, here], (own, LANES))
            cross_ref[:, here] = cross[:, p * LANES : (p + 1) * LANES] + (shift_ref[...] + line)
        return unused

    lax.fori_loop(0, total // width, fill, 0)


def final_kernel(sizes, *refs):
    n = len(sizes)
    crosses, stacks, gs = refs[:n], refs[n : 2 * n], refs[2 * n : -4]
    out_ref, shift_ref, high_ref, low_ref = refs[-4:]
    tall = high_ref.shape[1]
    segments = []
    col = first = 0
    for size, cross_ref, stack_ref in zip(sizes, crosses, stacks):
        base = col
        for side in range(2):
            for g in gs[first : first + size]:
                for k in range(g.shape[1]):
                    shift_ref[:, col : col + LANES] = jnp.broadcast_to(
                        g[side, k : k + 1, :], (8, LANES)
                    )
                    col += LANES
        first += size

        def make(span, k, cross_ref=cross_ref, base=base):
            line = jnp.broadcast_to(shift_ref[0:1, base + k : base + k + LANES], (tall, LANES))
            return jnp.exp2(cross_ref[span, k : k + LANES] + line)

        segments.append((make, stack_ref))
    weigh(segments, high_ref, low_ref, out_ref, None, crosses[0].shape[0])


def pairs(size, step):
    return [(k, k ^ step) for k in range(size)]


def swap(value, axis, step):
    return lax.ppermute(value, axis, pairs(lax.axis_size(axis), step))


def params(mib):
    return pltpu.CompilerParams(vmem_limit_bytes=mib << 20)


def in_vmem(value):
    return pltpu.with_memory_space_constraint(value, pltpu.VMEM)


def in_hbm(value):
    return pltpu.with_memory_space_constraint(value, pltpu.HBM)


def shards(source_pca, target_pca, source_labels, target_labels, block_mask):
    dims, rows = source_pca.shape
    cols = target_pca.shape[1]
    nsrc, ntgt = lax.axis_size("src"), lax.axis_size("tgt")
    total_rows, total_cols = rows * nsrc, cols * ntgt
    kappa = LOG2E / EPSILON
    scale, eps_scale = 2.0 * kappa / dims, kappa / dims
    xl, yl = source_labels.reshape(1, rows), target_labels.reshape(1, cols)
    row_lines, col_lines = (rows // LANES, LANES), (cols // LANES, LANES)
    depth = 3 * dims + block_mask.shape[0]
    sds = jax.ShapeDtypeStruct

    steps = list(range(2, ntgt, 2))
    third = max(1, len(steps) // 3)
    legs = [[0], steps[:third], steps[third : 2 * third], steps[2 * third :]]
    near, far = [], []
    for ks in legs:
        near.append([swap(target_pca, "tgt", k) if k else target_pca for k in ks])
        far.append([swap(y, "tgt", 1) for y in near[-1]])

    cross, lse, xsq = pl.pallas_call(
        functools.partial(first_kernel, scale, eps_scale),
        out_shape=(
            pltpu.VMEM((cols, rows), F32),
            sds((row_lines[0] + col_lines[0], LANES), F32),
            sds(row_lines, F32),
        ),
        out_specs=(VMEM,) * 3,
        in_specs=[HBM] * 5,
        scratch_shapes=[
            pltpu.VMEM((dims, rows), F32),
            pltpu.VMEM((dims, cols), F32),
            pltpu.VMEM((1, rows), jnp.int32),
            pltpu.VMEM((1, cols), jnp.int32),
            pltpu.VMEM(block_mask.shape, jnp.int32),
            pltpu.VMEM((cols, depth), BF16),
            pltpu.VMEM((cols, LANES), F32),
            pltpu.SemaphoreType.DMA((5,)),
        ],
        compiler_params=params(12),
        name="first",
    )(*map(in_hbm, (source_pca, target_pca, xl, yl, block_mask)))

    own = rows // ntgt
    xst, xop = pl.pallas_call(
        functools.partial(stack_kernel, scale),
        out_shape=(sds((2 * dims + 16, rows), BF16), sds((own, depth), BF16)),
        out_specs=(VMEM, VMEM),
        in_specs=[HBM] * 3,
        scratch_shapes=[
            pltpu.VMEM((dims, rows), F32),
            pltpu.VMEM((dims, own), F32),
            pltpu.VMEM((1, own), jnp.int32),
            pltpu.VMEM(block_mask.shape, jnp.int32),
            pltpu.SemaphoreType.DMA((4,)),
        ],
        compiler_params=params(8),
        name="stack",
    )(in_hbm(source_pca), in_hbm(xl), in_hbm(block_mask))

    def rows_parts(value, combine):
        other = swap(value, "tgt", 1)
        lines = row_lines[0]
        both = combine([value[:lines], other[:lines]])
        if value.shape[0] > lines:
            both = jnp.concatenate([both, value[lines:], other[lines:]], 0)
        return {0: both} | {k: swap(both, "tgt", k) for k in steps}

    def cols_parts(value):
        return [value] + [swap(value, "src", k) for k in range(1, nsrc)]

    add = functools.partial(tree, jnp.add)
    labelled = rows_parts(lse, merge)
    parts = list(labelled.values())
    col_lse, pots = pl.pallas_call(
        functools.partial(col_kernel, total_rows, len(parts)),
        out_shape=(sds(col_lines, F32), sds(row_lines, F32)),
        out_specs=(VMEM, VMEM),
        in_specs=[VMEM] * (2 + len(parts)),
        scratch_shapes=[
            pltpu.VMEM((8, rows), F32),
            pltpu.VMEM((cols, LANES), F32),
            pltpu.VMEM((cols, LANES), F32),
        ],
        compiler_params=params(8),
        name="col",
    )(in_vmem(cross), xsq, *parts)
    parts = cols_parts(col_lse)
    plan, sums, g = pl.pallas_call(
        functools.partial(row_kernel, total_cols, len(parts)),
        out_shape=(pltpu.VMEM((cols, rows), F32), sds(row_lines, F32), sds(col_lines, F32)),
        out_specs=(VMEM,) * 3,
        in_specs=[VMEM] * (2 + len(parts)),
        scratch_shapes=[pltpu.VMEM((cols, LANES), F32)],
        input_output_aliases={0: 0},
        compiler_params=params(8),
        name="row",
    )(in_vmem(cross), pots, *parts)
    parts = list(rows_parts(sums, add).values())
    mass, weight = pl.pallas_call(
        functools.partial(last_col_kernel, total_rows, len(parts)),
        out_shape=(sds(col_lines, F32), sds((dims, cols), F32)),
        out_specs=(VMEM, VMEM),
        in_specs=[VMEM] * (2 + len(parts)),
        scratch_shapes=[
            pltpu.VMEM((8, rows), F32),
            pltpu.VMEM((2 * dims + 16, min(256, cols)), F32),
            pltpu.VMEM((dims + 16, min(256, cols)), F32),
        ],
        compiler_params=params(8),
        name="last_col",
    )(in_vmem(plan), xst, *parts)
    mass = add(cols_parts(mass))
    weights = [weight] + [swap(weight, "src", k) for k in range(1, nsrc)]
    pot = g - math.log2(total_cols) - jnp.log2(mass)

    crosses, stacks, sizes = [], [], [len(ks) for ks in legs]
    for leg, ks in enumerate(legs):
        width = 2 * len(ks) * cols
        own_cross, stack = pl.pallas_call(
            functools.partial(ready_kernel, eps_scale, len(ks), row_lines[0]),
            out_shape=(pltpu.VMEM((own, width), F32), sds((2 * dims + 16, width), BF16)),
            out_specs=(VMEM, VMEM),
            in_specs=[VMEM] * (2 + 3 * len(ks)),
            scratch_shapes=[
                pltpu.VMEM((depth, width), BF16),
                pltpu.VMEM((8, width), F32),
                pltpu.VMEM((own, LANES), F32),
            ],
            compiler_params=params(4 + (width * (2 * depth + 32) >> 20)),
            name="ready",
        )(xop, pots, *near[leg], *far[leg], *[labelled[k] for k in ks])
        crosses.append(in_vmem(own_cross))
        stacks.append(stack)

    both = jnp.stack([pot, swap(pot, "tgt", 1)])
    gs = [both] + [swap(both, "tgt", k) for k in range(2, ntgt, 2)]
    source_projection = pl.pallas_call(
        functools.partial(final_kernel, sizes),
        out_shape=sds((dims, own), F32),
        out_specs=VMEM,
        in_specs=[VMEM] * (2 * len(sizes) + len(gs)),
        scratch_shapes=[
            pltpu.VMEM((8, total_cols), F32),
            pltpu.VMEM((2 * dims + 16, min(256, own)), F32),
            pltpu.VMEM((dims + 16, min(256, own)), F32),
        ],
        compiler_params=params(8),
        name="final",
    )(*crosses, *stacks, *gs)
    target_projection = add(weights) / mass.reshape(1, cols)
    return (source_projection, target_projection)


def solution(mesh):
    placed = (P(None, "src"), P(None, "tgt"), P("src"), P("tgt"), P())
    return jax.shard_map(
        shards,
        mesh=mesh,
        in_specs=placed,
        out_specs=(P(None, ("src", "tgt")), P(None, "tgt")),
        check_vma=False,
    )
```

```python
import functools
import math

import jax
import jax.numpy as jnp
from jax import lax
from jax.experimental import pallas as pl
from jax.experimental.pallas import tpu as pltpu
from jax.sharding import PartitionSpec as P

EPSILON = 0.05
BARRED = -(2.0**100)
LANES = 128
LOG2E = math.log2(math.e)
F32 = jnp.float32
BF16 = jnp.bfloat16
VMEM = pl.BlockSpec(memory_space=pltpu.VMEM)
HBM = pl.BlockSpec(memory_space=pltpu.HBM)


def halves(value):
    high = value.astype(BF16)
    low = (value - high.astype(F32)).astype(BF16)
    return high, low


def onehot(labels, clusters):
    series = lax.broadcasted_iota(jnp.int32, (clusters, labels.shape[1]), 0)
    return series == labels


def barred_by(mask_ref, hot, transposed):
    stop = (1.0 - mask_ref[...].astype(F32)).astype(BF16)
    dims = (((0,), (0,)), ((), ())) if transposed else (((1,), (0,)), ((), ()))
    picked = lax.dot_general(stop, hot.astype(BF16), dims, preferred_element_type=F32)
    return picked * BARRED


def tree(combine, parts):
    parts = list(parts)
    while len(parts) > 1:
        parts = [
            combine(parts[k], parts[k + 1]) if k + 1 < len(parts) else parts[k]
            for k in range(0, len(parts), 2)
        ]
    return parts[0]


def merge(tops):
    peak = tree(jnp.maximum, tops)
    return peak + jnp.log2(tree(jnp.add, [jnp.exp2(part - peak) for part in tops]))


def spread_lanes(dst_ref, rows):
    for k in range(rows.shape[0]):
        square = jnp.broadcast_to(rows[k : k + 1, :], (LANES, LANES))
        dst_ref[k * LANES : (k + 1) * LANES, :] = square.T


def gather_lanes(dst_ref, column_ref):
    for k in range(dst_ref.shape[0]):
        dst_ref[k : k + 1, :] = column_ref[k * LANES : (k + 1) * LANES, :].T[0:1, :]


def online(peak, total, z):
    newer = jnp.maximum(peak, tree(jnp.maximum, z))
    fresh = tree(jnp.add, [jnp.exp2(part - newer) for part in z])
    return newer, total * jnp.exp2(peak - newer) + fresh


def down(peak, total):
    top = jnp.max(peak, 0, keepdims=True)
    return top + jnp.log2(jnp.sum(total * jnp.exp2(peak - top), 0, keepdims=True))


def fetch(pairs, sems):
    copies = [pltpu.make_async_copy(src, dst, sems.at[k]) for k, (src, dst) in enumerate(pairs)]
    for copy in copies:
        copy.start()
    return copies


def first_kernel(
    scale, eps_scale, x_hbm, y_hbm, sl_hbm, tl_hbm, mask_hbm,
    cross_ref, lse_ref, xsq_ref,
    x_ref, y_ref, sl_ref, tl_ref, mask_ref, yop_ref, ysq_ref, sems,
):
    copies = fetch(
        [(y_hbm, y_ref), (tl_hbm, tl_ref), (mask_hbm, mask_ref), (sl_hbm, sl_ref), (x_hbm, x_ref)],
        sems,
    )
    _, rows = x_ref.shape
    cols = y_ref.shape[1]
    clusters = mask_ref.shape[0]
    for copy in copies[:3]:
        copy.wait()
    high, low = halves(y_ref[...] * scale)
    barred = barred_by(mask_ref, onehot(tl_ref[...], clusters), False)
    stacked = jnp.concatenate([high.astype(F32), high.astype(F32), low.astype(F32), barred], 0)
    yop_ref[...] = stacked.T.astype(BF16)
    ysq = jnp.sum(y_ref[...] * y_ref[...], 0, keepdims=True) * (-eps_scale)
    for k in range(cols // LANES):
        square = jnp.broadcast_to(ysq[:, k * LANES : (k + 1) * LANES], (LANES, LANES))
        ysq_ref[k * LANES : (k + 1) * LANES, :] = square.T
    for copy in copies[3:]:
        copy.wait()
    width = min(1024, rows)
    narrow = min(256, width)
    depth = min(32, cols)
    base = rows // LANES
    for k in range(cols // LANES):
        lse_ref[base + k : base + k + 1, :] = tl_ref[:, k * LANES : (k + 1) * LANES].astype(F32)

    def chunk(q, unused):
        base = pl.multiple_of(q * width, width)
        here = cross_ref.at[:, pl.ds(base, width)]
        xs = x_ref.at[:, pl.ds(base, width)]
        labels = sl_ref.at[:, pl.ds(base, width)]
        per = narrow // LANES
        for n in range(0, width, narrow):
            x = xs[:, n : n + narrow]
            high, low = halves(x)
            hot = onehot(labels[:, n : n + narrow], clusters).astype(BF16)
            xop = jnp.concatenate([high, low, high, hot], 0)
            xsq = jnp.sum(x * x, 0, keepdims=True) * eps_scale
            cross = jnp.dot(yop_ref[...], xop, preferred_element_type=F32)
            peaks = [jnp.full((8, LANES), 2.0 * BARRED, F32)] * per
            totals = [jnp.zeros((8, LANES), F32)] * per
            for top in range(0, cols, depth):
                for p in range(per):
                    z = []
                    for r in range(top, top + depth, 8):
                        z.append(cross[r : r + 8, p * LANES : (p + 1) * LANES] + ysq_ref[r : r + 8, :])
                        here[r : r + 8, n + p * LANES : n + (p + 1) * LANES] = z[-1]
                    peaks[p], totals[p] = online(peaks[p], totals[p], z)
            for p in range(per):
                line = pl.ds(q * (width // LANES) + n // LANES + p, 1)
                xsq_ref[line, :] = xsq[:, p * LANES : (p + 1) * LANES]
                lse_ref[line, :] = down(peaks[p], totals[p])
        return unused

    lax.fori_loop(0, rows // width, chunk, 0)


def source_shift(parts_refs, xsq_ref, total_rows):
    lines = xsq_ref.shape[0]
    lse = merge([ref[0:lines, :] for ref in parts_refs]) - xsq_ref[...]
    pot = -math.log2(total_rows) - lse
    return pot - xsq_ref[...]


def target_potential(parts_refs, total_cols):
    return -math.log2(total_cols) - merge([ref[...] for ref in parts_refs])


def spread_rows(shift_ref, shift):
    for k in range(shift.shape[0]):
        shift_ref[:, k * LANES : (k + 1) * LANES] = jnp.broadcast_to(shift[k : k + 1, :], (8, LANES))


def col_kernel(total_rows, n_parts, cross_ref, xsq_ref, *refs):
    parts, (lse_ref, pot_ref, shift_ref, peak_ref, mass_ref) = refs[:n_parts], refs[n_parts:]
    cols, rows = cross_ref.shape
    pot_ref[...] = source_shift(parts, xsq_ref, total_rows)
    spread_rows(shift_ref, pot_ref[...])
    deep = min(16, rows // LANES)
    groups = 8

    def block(q, unused):
        for r in range(groups):
            start = pl.ds(pl.multiple_of((q * groups + r) * 8, 8), 8)
            peak = jnp.full((8, LANES), 2.0 * BARRED, F32)
            total = jnp.zeros((8, LANES), F32)
            for c in range(0, rows // LANES, deep):
                lanes = [slice(k * LANES, (k + 1) * LANES) for k in range(c, c + deep)]
                z = [cross_ref[start, at] + shift_ref[:, at] for at in lanes]
                peak, total = online(peak, total, z)
            peak_ref[start, :] = peak
            mass_ref[start, :] = total
        return unused

    lax.fori_loop(0, cols // 8 // groups, block, 0)
    peak = peak_ref[...]
    top = jnp.max(peak, 1, keepdims=True)
    mass = jnp.sum(mass_ref[...] * jnp.exp2(peak - top), 1, keepdims=True)
    mass_ref[...] = jnp.broadcast_to(top + jnp.log2(mass), mass_ref.shape)
    gather_lanes(lse_ref, mass_ref)


def row_kernel(total_cols, n_parts, cross_ref, pot_ref, *refs):
    parts, (plan_ref, sums_ref, g_ref, shift_ref) = refs[:n_parts], refs[n_parts:]
    g_ref[...] = target_potential(parts, total_cols)
    spread_lanes(shift_ref, g_ref[...])
    cols, rows = plan_ref.shape
    width = min(512, rows)

    def block(q, unused):
        tiles = range(width // LANES)
        here = plan_ref.at[:, pl.ds(pl.multiple_of(q * width, width), width)]
        lines = q * (width // LANES)
        pot = [jnp.broadcast_to(pot_ref[pl.ds(lines + p, 1), :], (8, LANES)) for p in tiles]
        totals = [[] for p in tiles]
        for start in range(0, cols, 32):
            t = [[] for p in tiles]
            for r in range(start, start + 32, 8):
                for p in tiles:
                    at = slice(p * LANES, (p + 1) * LANES)
                    part = jnp.exp2(here[r : r + 8, at] + (shift_ref[r : r + 8, :] + pot[p]))
                    here[r : r + 8, at] = part
                    t[p].append(part)
            for p in tiles:
                totals[p] = [tree(jnp.add, totals[p] + t[p])]
        for p in tiles:
            sums_ref[pl.ds(lines + p, 1), :] = jnp.sum(totals[p][0], 0, keepdims=True)
        return unused

    lax.fori_loop(0, rows // width, block, 0)


def weigh(segments, high_ref, low_ref, out_ref, mass_ref, rows):
    dims = out_ref.shape[0]
    tall = high_ref.shape[1]
    short = low_ref.shape[0]
    lanes = (((1,), (1,)), ((), ()))

    def block(q, unused):
        span = pl.ds(pl.multiple_of(q * tall, tall), tall)
        first = True
        for make, stack_ref in segments:
            width = stack_ref.shape[1]
            deep = min(1024, width)
            for c in range(0, width, deep):
                highs, lows = [], []
                for k in range(c, c + deep, LANES):
                    high, low = halves(make(span, k))
                    highs.append(high)
                    lows.append(low)
                stack = stack_ref[:, c : c + deep]
                with_high = lax.dot_general(
                    stack, jnp.concatenate(highs, 1), lanes, preferred_element_type=F32
                )
                with_low = lax.dot_general(
                    stack[:short], jnp.concatenate(lows, 1), lanes, preferred_element_type=F32
                )
                if first:
                    high_ref[...] = with_high
                    low_ref[...] = with_low
                else:
                    high_ref[...] += with_high
                    low_ref[...] += with_low
                first = False
        mass = high_ref[dims : dims + 1, :] + low_ref[dims : dims + 1, :]
        weight = (high_ref[:dims, :] + low_ref[:dims, :]) + high_ref[short:, :]
        if mass_ref is None:
            weight = weight / mass
        else:
            for k in range(tall // LANES):
                line = pl.ds(q * (tall // LANES) + k, 1)
                mass_ref[line, :] = mass[:, k * LANES : (k + 1) * LANES]
        out_ref[:, span] = weight
        return unused

    lax.fori_loop(0, rows // tall, block, 0)


def stack_lines(stack_ref, at, high, low):
    _, n = high.shape
    stack_ref[:, at] = jnp.concatenate([high, jnp.ones((16, n), BF16), low], 0)


def stack_kernel(
    scale, x_hbm, sl_hbm, mask_hbm, xst_ref, xop_ref, x_ref, own_ref, sl_ref, mask_ref, sems
):
    own, rows = xop_ref.shape[1], x_ref.shape[1]
    start = pl.multiple_of(lax.axis_index("tgt") * own, own)
    mine = pl.ds(start, own)
    copies = fetch(
        [
            (x_hbm.at[:, mine], own_ref),
            (sl_hbm.at[:, mine], sl_ref),
            (mask_hbm, mask_ref),
            (x_hbm, x_ref),
        ],
        sems,
    )
    clusters = mask_ref.shape[0]
    for copy in copies[:3]:
        copy.wait()
    high, low = halves(own_ref[...] * scale)
    barred = barred_by(mask_ref, onehot(sl_ref[...], clusters), True)
    xop_ref[...] = jnp.concatenate([high, low, high, barred.astype(BF16)], 0)
    copies[3].wait()
    step = min(512, rows)
    for k in range(0, rows, step):
        stack_lines(xst_ref, slice(k, k + step), *halves(x_ref[:, k : k + step]))


def last_col_kernel(total_rows, n_parts, plan_ref, xst_ref, *refs):
    parts = refs[:n_parts]
    sums_ref, weight_ref, scale_ref, high_ref, low_ref = refs[n_parts:]
    cols = plan_ref.shape[0]
    tall = high_ref.shape[1]
    spread_rows(scale_ref, 1.0 / (total_rows * tree(jnp.add, [ref[...] for ref in parts])))

    def make(span, k):
        line = jnp.broadcast_to(scale_ref[0:1, k : k + LANES], (tall, LANES))
        return plan_ref[span, k : k + LANES] * line

    weigh([(make, xst_ref)], high_ref, low_ref, weight_ref, sums_ref, cols)


def ready_kernel(eps_scale, n_near, lines, xop_ref, pot_ref, *refs):
    near, far, labels = refs[:n_near], refs[n_near : 2 * n_near], refs[2 * n_near : 3 * n_near]
    cross_ref, yst_ref, square_ref, yop_ref = refs[3 * n_near :]
    total, own = cross_ref.shape
    dims, cols = near[0].shape
    clusters = yop_ref.shape[1] - 3 * dims
    tiles = cols // LANES
    for n, ref in enumerate(near + far):
        at = slice(n * cols, (n + 1) * cols)
        y = ref[...]
        high, low = halves(y)
        stack_lines(yst_ref, at, high, low)
        side, which = divmod(n, n_near)
        hots = []
        for k in range(tiles):
            line = lines + side * tiles + k
            label = labels[which][line : line + 1, :].astype(jnp.int32)
            hots.append(onehot(label, clusters).astype(F32))
        ysq = jnp.sum(y * y, 0, keepdims=True) * eps_scale
        for k in range(tiles):
            square_ref[n * tiles + k : n * tiles + k + 1, :] = ysq[:, k * LANES : (k + 1) * LANES]
        high, low = high.astype(F32), low.astype(F32)
        stacked = jnp.concatenate([high, high, low, jnp.concatenate(hots, 1)], 0)
        yop_ref[at, :] = stacked.T.astype(BF16)
    place = lax.axis_index("tgt") * (own // LANES)
    pots = [pot_ref[pl.ds(place + p, 1), :] for p in range(own // LANES)]
    tall = min(1024, total)

    def fill(q, unused):
        here = pl.ds(pl.multiple_of(q * tall, tall), tall)
        cross = jnp.dot(yop_ref[here, :], xop_ref[...], preferred_element_type=F32)
        for p in range(own // LANES):
            lanes = slice(p * LANES, (p + 1) * LANES)
            cross_ref[here, lanes] = cross[:, lanes] + jnp.broadcast_to(pots[p], (tall, LANES))
        return unused

    lax.fori_loop(0, total // tall, fill, 0)


def final_kernel(sizes, *refs):
    n = len(sizes)
    crosses, stacks, squares, gs = refs[:n], refs[n : 2 * n], refs[2 * n : 3 * n], refs[3 * n : -3]
    out_ref, high_ref, low_ref = refs[-3:]
    dims, own = out_ref.shape
    short = low_ref.shape[0]
    first, base = True, 0
    for size, cross_ref, stack_ref, square_ref in zip(sizes, crosses, stacks, squares):
        g = [
            ref[side, k : k + 1, :]
            for side in range(2)
            for ref in gs[base : base + size]
            for k in range(ref.shape[1])
        ]
        base += size
        deep = min(1024, cross_ref.shape[0])
        for c in range(0, cross_ref.shape[0], deep):
            highs, lows = [], []
            for r in range(c, c + deep, LANES):
                k = r // LANES
                line = g[k] - square_ref[k : k + 1, :]
                shift = jnp.broadcast_to(line, (LANES, LANES)).T
                parts = [
                    halves(jnp.exp2(cross_ref[r : r + LANES, p : p + LANES] + shift))
                    for p in range(0, own, LANES)
                ]
                highs.append(jnp.concatenate([part[0] for part in parts], 1))
                lows.append(jnp.concatenate([part[1] for part in parts], 1))
            stack = stack_ref[:, c : c + deep]
            with_high = jnp.dot(stack, jnp.concatenate(highs, 0), preferred_element_type=F32)
            with_low = jnp.dot(stack[:short], jnp.concatenate(lows, 0), preferred_element_type=F32)
            if first:
                high_ref[...] = with_high
                low_ref[...] = with_low
            else:
                high_ref[...] += with_high
                low_ref[...] += with_low
            first = False
    mass = high_ref[dims : dims + 1, :] + low_ref[dims : dims + 1, :]
    weight = (high_ref[:dims, :] + low_ref[:dims, :]) + high_ref[short:, :]
    out_ref[...] = weight / mass


def pairs(size, step):
    return [(k, k ^ step) for k in range(size)]


def swap(value, axis, step):
    return lax.ppermute(value, axis, pairs(lax.axis_size(axis), step))


def params(mib):
    return pltpu.CompilerParams(vmem_limit_bytes=mib << 20)


def in_vmem(value):
    return pltpu.with_memory_space_constraint(value, pltpu.VMEM)


def in_hbm(value):
    return pltpu.with_memory_space_constraint(value, pltpu.HBM)


def shards(source_pca, target_pca, source_labels, target_labels, block_mask):
    dims, rows = source_pca.shape
    cols = target_pca.shape[1]
    nsrc, ntgt = lax.axis_size("src"), lax.axis_size("tgt")
    total_rows, total_cols = rows * nsrc, cols * ntgt
    kappa = LOG2E / EPSILON
    scale, eps_scale = 2.0 * kappa / dims, kappa / dims
    xl, yl = source_labels.reshape(1, rows), target_labels.reshape(1, cols)
    row_lines, col_lines = (rows // LANES, LANES), (cols // LANES, LANES)
    depth = 3 * dims + block_mask.shape[0]
    sds = jax.ShapeDtypeStruct

    steps = list(range(2, ntgt, 2))
    third = max(1, len(steps) // 3)
    legs = [[0], steps[:third], steps[third : 2 * third], steps[2 * third :]]
    near, far = [], []
    for ks in legs:
        near.append([swap(target_pca, "tgt", k) if k else target_pca for k in ks])
        far.append([swap(y, "tgt", 1) for y in near[-1]])

    cross, lse, xsq = pl.pallas_call(
        functools.partial(first_kernel, scale, eps_scale),
        out_shape=(
            pltpu.VMEM((cols, rows), F32),
            sds((row_lines[0] + col_lines[0], LANES), F32),
            sds(row_lines, F32),
        ),
        out_specs=(VMEM,) * 3,
        in_specs=[HBM] * 5,
        scratch_shapes=[
            pltpu.VMEM((dims, rows), F32),
            pltpu.VMEM((dims, cols), F32),
            pltpu.VMEM((1, rows), jnp.int32),
            pltpu.VMEM((1, cols), jnp.int32),
            pltpu.VMEM(block_mask.shape, jnp.int32),
            pltpu.VMEM((cols, depth), BF16),
            pltpu.VMEM((cols, LANES), F32),
            pltpu.SemaphoreType.DMA((5,)),
        ],
        compiler_params=params(12),
        name="first",
    )(*map(in_hbm, (source_pca, target_pca, xl, yl, block_mask)))

    own = rows // ntgt
    xst, xop = pl.pallas_call(
        functools.partial(stack_kernel, scale),
        out_shape=(sds((2 * dims + 16, rows), BF16), sds((depth, own), BF16)),
        out_specs=(VMEM, VMEM),
        in_specs=[HBM] * 3,
        scratch_shapes=[
            pltpu.VMEM((dims, rows), F32),
            pltpu.VMEM((dims, own), F32),
            pltpu.VMEM((1, own), jnp.int32),
            pltpu.VMEM(block_mask.shape, jnp.int32),
            pltpu.SemaphoreType.DMA((4,)),
        ],
        compiler_params=params(8),
        name="stack",
    )(in_hbm(source_pca), in_hbm(xl), in_hbm(block_mask))

    def rows_parts(value, combine):
        other = swap(value, "tgt", 1)
        lines = row_lines[0]
        both = combine([value[:lines], other[:lines]])
        if value.shape[0] > lines:
            both = jnp.concatenate([both, value[lines:], other[lines:]], 0)
        return {0: both} | {k: swap(both, "tgt", k) for k in steps}

    def cols_parts(value):
        return [value] + [swap(value, "src", k) for k in range(1, nsrc)]

    add = functools.partial(tree, jnp.add)
    labelled = rows_parts(lse, merge)
    parts = list(labelled.values())
    col_lse, pots = pl.pallas_call(
        functools.partial(col_kernel, total_rows, len(parts)),
        out_shape=(sds(col_lines, F32), sds(row_lines, F32)),
        out_specs=(VMEM, VMEM),
        in_specs=[VMEM] * (2 + len(parts)),
        scratch_shapes=[
            pltpu.VMEM((8, rows), F32),
            pltpu.VMEM((cols, LANES), F32),
            pltpu.VMEM((cols, LANES), F32),
        ],
        compiler_params=params(8),
        name="col",
    )(in_vmem(cross), xsq, *parts)
    parts = cols_parts(col_lse)
    plan, sums, g = pl.pallas_call(
        functools.partial(row_kernel, total_cols, len(parts)),
        out_shape=(pltpu.VMEM((cols, rows), F32), sds(row_lines, F32), sds(col_lines, F32)),
        out_specs=(VMEM,) * 3,
        in_specs=[VMEM] * (2 + len(parts)),
        scratch_shapes=[pltpu.VMEM((cols, LANES), F32)],
        input_output_aliases={0: 0},
        compiler_params=params(8),
        name="row",
    )(in_vmem(cross), pots, *parts)
    parts = list(rows_parts(sums, add).values())
    mass, weight = pl.pallas_call(
        functools.partial(last_col_kernel, total_rows, len(parts)),
        out_shape=(sds(col_lines, F32), sds((dims, cols), F32)),
        out_specs=(VMEM, VMEM),
        in_specs=[VMEM] * (2 + len(parts)),
        scratch_shapes=[
            pltpu.VMEM((8, rows), F32),
            pltpu.VMEM((2 * dims + 16, min(256, cols)), F32),
            pltpu.VMEM((dims + 16, min(256, cols)), F32),
        ],
        compiler_params=params(8),
        name="last_col",
    )(in_vmem(plan), xst, *parts)
    mass = add(cols_parts(mass))
    weights = [weight] + [swap(weight, "src", k) for k in range(1, nsrc - 1)]
    weights.append(swap(weight, "src", nsrc - 1))
    pot = g - math.log2(total_cols) - jnp.log2(mass)

    crosses, stacks, squares, sizes = [], [], [], [len(ks) for ks in legs]
    for leg, ks in enumerate(legs):
        width = 2 * len(ks) * cols
        own_cross, stack, square = pl.pallas_call(
            functools.partial(ready_kernel, eps_scale, len(ks), row_lines[0]),
            out_shape=(
                pltpu.VMEM((width, own), F32),
                sds((2 * dims + 16, width), BF16),
                sds((width // LANES, LANES), F32),
            ),
            out_specs=(VMEM,) * 3,
            in_specs=[VMEM] * (2 + 3 * len(ks)),
            scratch_shapes=[pltpu.VMEM((width, depth), BF16)],
            compiler_params=params(6 + (width * 2 * depth >> 20)),
            name="ready",
        )(xop, pots, *near[leg], *far[leg], *[labelled[k] for k in ks])
        crosses.append(in_vmem(own_cross))
        stacks.append(stack)
        squares.append(square)

    both = jnp.stack([pot, swap(pot, "tgt", 1)])
    gs = [both] + [swap(both, "tgt", k) for k in range(2, ntgt, 2)]
    source_projection = pl.pallas_call(
        functools.partial(final_kernel, sizes),
        out_shape=sds((dims, own), F32),
        out_specs=VMEM,
        in_specs=[VMEM] * (3 * len(sizes) + len(gs)),
        scratch_shapes=[pltpu.VMEM((2 * dims + 16, own), F32), pltpu.VMEM((dims + 16, own), F32)],
        compiler_params=params(8),
        name="final",
    )(*crosses, *stacks, *squares, *gs)
    target_projection = add(weights) / mass.reshape(1, cols)
    return (source_projection, target_projection)


def solution(mesh):
    placed = (P(None, "src"), P(None, "tgt"), P("src"), P("tgt"), P())
    return jax.shard_map(
        shards,
        mesh=mesh,
        in_specs=placed,
        out_specs=(P(None, ("src", "tgt")), P(None, "tgt")),
        check_vma=False,
    )
```
